32 devices in a mesh: cols: 16 (over z, y, x), params: 2 (over core).
Axes of the slice: x: 2, y: 2, z: 4, core: 2. Of those that a mesh axis runs over, the one named last changes fastest.
Arguments:
- concentration: float32 [128, 16384], P(None, ('cols', 'params')), may hold values from 0.2 to 5
- emissions: float32 [128, 16384], P(None, ('cols', 'params')), may hold values from 0 to 1
- rate_table: float32 [8, 16, 16], replicated, may hold values from 0.01 to 0.3
- species_order: int32 [128], replicated, may hold values from 0 to 127, each once
- sensitivity: float32 [4, 128, 32, 4, 128], P('params', None, 'cols'), may hold values from -6 to 6
- source_terms: bfloat16 [4, 128, 32, 4, 128], P('params', None, 'cols'), may hold values from 0 to 2
- courant_x: float32 [32, 4, 128], P('cols'), may hold values from 0.05 to 0.24
- upwind_x: int32 [32, 4, 128], P('cols'), may hold values from 0 to 1
- courant_y: float32 [32, 4, 128], P('cols'), may hold values from 0.05 to 0.24
- upwind_y: int32 [32, 4, 128], P('cols'), may hold values from 0 to 1
Outputs:
- new_concentration: float32 [128, 16384], P(None, ('cols', 'params'))
- new_sensitivity: float32 [4, 128, 32, 4, 128], P('params', None, 'cols')
- sensitivity_burden: float32 [4, 128], P('params')
- species_burden: float32 [128], replicated
The draws below stay inside these ranges and needn't reach their ends.
Inputs may be any that keep to these rules, and one draw needn't show every extreme that they name: `species_order`: each species appears exactly once. `upwind_x`: 1 means the wind blows toward higher indices through the face. `upwind_y`: 1 means the wind blows toward higher indices through the face.
All inputs are finite; a program needn't handle non-finite values.
Results may differ from the reference program's by a relative error of at most 0.0016.
Values may be sent and summed in bfloat16 or wider, within the bound.
A program may use at most 128 MiB of HBM per device.

```python
import math
import jax
import jax.numpy as jnp
from jax import lax

SPECIES = 128
BLOCK = 16
LAYERS = 4
TY = 128
SUBSTEPS = 2
NBLOCK = 8
NPARAM = 4
NX = 32
NCELL = 16384


def touch_ends(values, rng, least, top_value):
    spot = [jax.random.randint(jax.random.fold_in(rng, axis), (), 0, length) for axis, length in enumerate(values.shape)]
    longest = values.shape.index(max(values.shape))
    beside = spot[:longest] + [(spot[longest] + 1) % values.shape[longest]] + spot[longest + 1:]
    return values.at[tuple(spot)].set(least).at[tuple(beside)].set(top_value)


def block_levels(key, dims, shards, smallest, largest):
    gain = 1.0
    for axis_at, blocks in shards:
        steps = jax.random.uniform(jax.random.fold_in(jax.random.fold_in(key, 6), axis_at), (blocks,), jnp.float32, smallest / len(shards), largest / len(shards))
        gain = gain * jnp.repeat(jnp.exp(steps), dims[axis_at] // blocks).reshape((-1,) + (1,) * (len(dims) - 1 - axis_at))
    return gain


def gaussian(stream_key, extent, width, bound, pieces=(), held_as=jnp.bfloat16):
    entries = width * jax.random.normal(stream_key, extent, jnp.float32)
    if pieces:
        entries = entries * block_levels(stream_key, extent, pieces, -0.22, 0.18)
    return jnp.clip(entries, -bound, bound).astype(held_as)


def setup_inputs(seed: int = 0) -> dict:
    seeds = jax.random.split(jax.random.key(seed), 11)
    return {
        "concentration": jnp.clip(jnp.exp(math.log(5.0) - 3.218876 * jax.random.uniform(seeds[0], (SPECIES, NCELL), jnp.float32) ** block_levels(seeds[0], (SPECIES, NCELL), ((1, 32),), -0.2, 0.2)), 0.2, 5.0),
        "emissions": jnp.clip(1.0 * jax.random.uniform(seeds[1], (SPECIES, NCELL), jnp.float32) ** block_levels(seeds[1], (SPECIES, NCELL), ((1, 32),), -0.2, 0.2), 0.0, 1.0),
        "rate_table": jnp.clip(jnp.exp(jax.random.uniform(seeds[2], (NBLOCK, BLOCK, BLOCK), jnp.float32, math.log(0.01), math.log(0.3))), 0.01, 0.3),
        "species_order": jax.random.permutation(seeds[3], SPECIES).astype(jnp.int32),
        "sensitivity": gaussian(seeds[4], (NPARAM, SPECIES, NX, LAYERS, TY), 1.0, 6.0, ((0, 2), (2, 16)), jnp.float32),
        "source_terms": jnp.clip(2.0 * jax.random.uniform(seeds[5], (NPARAM, SPECIES, NX, LAYERS, TY), jnp.float32) ** block_levels(seeds[5], (NPARAM, SPECIES, NX, LAYERS, TY), ((0, 2), (2, 16)), -0.2, 0.2), 0.0, 2.0).astype(jnp.bfloat16),
        "courant_x": jnp.clip(0.05 + 0.19 * jax.random.uniform(seeds[6], (NX, LAYERS, TY), jnp.float32) ** block_levels(seeds[6], (NX, LAYERS, TY), ((0, 16),), -0.2, 0.2), 0.05, 0.24),
        "upwind_x": touch_ends(jax.random.randint(seeds[7], (NX, LAYERS, TY), 0, 2), jax.random.fold_in(seeds[7], 1), 0, 1).astype(jnp.int32),
        "courant_y": jnp.clip(0.05 + 0.19 * jax.random.uniform(seeds[8], (NX, LAYERS, TY), jnp.float32) ** block_levels(seeds[8], (NX, LAYERS, TY), ((0, 16),), -0.2, 0.2), 0.05, 0.24),
        "upwind_y": touch_ends(jax.random.randint(seeds[9], (NX, LAYERS, TY), 0, 2), jax.random.fold_in(seeds[9], 1), 0, 1).astype(jnp.int32),
    }


def invert_blocks(matrix):
    size = matrix.shape[1]
    positions = jnp.arange(size)

    def eliminate(pivot_index, current):
        pivot = 1.0 / current[:, pivot_index, pivot_index, :]
        pivot_row = current[:, pivot_index, :, :] * pivot[:, None, :]
        pivot_row = jnp.where((positions == pivot_index)[None, :, None], pivot[:, None, :], pivot_row)
        column = current[:, :, pivot_index, :]
        updated = current - column[:, :, None, :] * pivot_row[:, None, :, :]
        updated = jnp.where((positions == pivot_index)[None, None, :, None], -column[:, :, None, :] * pivot[:, None, None, :], updated)
        updated = jnp.where((positions == pivot_index)[None, :, None, None], pivot_row[:, None, :, :], updated)
        return updated

    return lax.fori_loop(0, size, eliminate, matrix)


def build_factors(conc_cells, species_order, rate_table):
    block_count, block_width = rate_table.shape[0], rate_table.shape[1]
    ordered = jnp.take(conc_cells, species_order, axis=0).reshape(block_count, block_width, -1)
    coupling = rate_table[:, :, :, None] * ordered[:, None, :, :]
    row_total = jnp.sum(coupling, axis=2)
    positions = jnp.arange(block_width)
    identity = (positions[:, None] == positions[None, :]).astype(jnp.float32)
    system = identity[None, :, :, None] * (1.0 + row_total)[:, :, None, :] - coupling
    return invert_blocks(system).astype(jnp.bfloat16)


def apply_blocks(factors, values):
    result = jnp.zeros(values.shape, jnp.float32)
    for column_index in range(factors.shape[2]):
        result = result + factors[:, :, column_index, :].astype(jnp.float32)[None] * values[:, :, column_index, :][:, :, None, :]
    return result


def advect(tracer, courant_x, upwind_x, courant_y, upwind_y):
    before_x = jnp.concatenate([jnp.zeros_like(tracer[:, :, :1]), tracer[:, :, :-1]], axis=2)
    lower_x = courant_x * jnp.where(upwind_x == 1, before_x, -tracer)
    upper_x = jnp.concatenate([lower_x[:, :, 1:], jnp.zeros_like(lower_x[:, :, :1])], axis=2)
    before_y = jnp.concatenate([jnp.zeros_like(tracer[..., :1]), tracer[..., :-1]], axis=4)
    lower_y = courant_y * jnp.where(upwind_y == 1, before_y, -tracer)
    upper_y = jnp.concatenate([lower_y[..., 1:], jnp.zeros_like(lower_y[..., :1])], axis=4)
    return tracer + lower_x - upper_x + lower_y - upper_y


def reference(concentration, emissions, rate_table, species_order, sensitivity, source_terms, courant_x, upwind_x, courant_y, upwind_y):
    block_count = SPECIES // BLOCK
    plane_cells = LAYERS * TY
    tracer = sensitivity
    for substep in range(SUBSTEPS):
        tracer = advect(tracer, courant_x, upwind_x, courant_y, upwind_y)
    inverse = jnp.argsort(species_order).astype(jnp.int32)
    right_side = jnp.take(tracer + source_terms.astype(jnp.float32), species_order, axis=1)
    right_side = right_side.reshape(NPARAM, block_count, BLOCK, NX, plane_cells).transpose(3, 0, 1, 2, 4)
    base_side = jnp.take(concentration + emissions, species_order, axis=0)
    base_side = base_side.reshape(block_count, BLOCK, NX, plane_cells).transpose(2, 0, 1, 3)
    conc_planes = concentration.reshape(SPECIES, NX, plane_cells).transpose(1, 0, 2)

    def one_plane(items):
        conc_plane, base_plane, side_plane = items
        factors = build_factors(conc_plane, species_order, rate_table)
        return apply_blocks(factors, base_plane[None])[0], apply_blocks(factors, side_plane)

    new_base, new_tracer = lax.map(one_plane, (conc_planes, base_side, right_side))
    new_base = new_base.transpose(1, 2, 0, 3).reshape(SPECIES, NCELL)
    new_concentration = jnp.take(new_base, inverse, axis=0)
    new_tracer = new_tracer.transpose(1, 2, 3, 0, 4).reshape(NPARAM, SPECIES, NX, LAYERS, TY)
    new_sensitivity = jnp.take(new_tracer, inverse, axis=1)
    sensitivity_burden = jnp.sum(new_sensitivity, axis=(2, 3, 4)) / NCELL
    species_burden = jnp.sum(new_concentration, axis=1) / NCELL
    return new_concentration, new_sensitivity, sensitivity_burden, species_burden
```

```python
import functools
import jax
import jax.numpy as jnp
from jax import lax
from jax.experimental import pallas as pl
from jax.experimental.pallas import tpu as pltpu
from jax.sharding import PartitionSpec as P

MESH = pl.DeviceIdType.MESH
SUB = 8


def one_hot(column_ref):
    species = column_ref.shape[0]
    at = lax.broadcasted_iota(jnp.int32, (species, species), 1)
    return jnp.where(at == column_ref[...], 1.0, 0.0).astype(jnp.float32)


def exact_dot(left, right, over):
    return lax.dot_general(
        left, right, (over, ((), ())),
        precision=lax.Precision.HIGHEST, preferred_element_type=jnp.float32,
    )


def order_kernel(order_ref, column_ref, conc_ref, emis_ref, sens_ref, src_ref, conc_o, emis_o, sens_o, src_o):
    turn = one_hot(column_ref)
    conc_o[...] = exact_dot(turn, conc_ref[...], ((1,), (0,)))
    emis_o[...] = exact_dot(turn, emis_ref[...], ((1,), (0,)))

    @pl.loop(0, sens_ref.shape[1], unroll=8)
    def _(k):
        at = order_ref[k]
        for g in range(2):
            sens_o[g, k] = sens_ref[g, at]
            src_o[g, k] = src_ref[g, at]


def restore_kernel(order_ref, column_ref, newc_o, news_o, burd_o, newc_ref, news_ref, sburd_ref, cburd_ref):
    turn = one_hot(column_ref)
    newc_ref[...] = exact_dot(turn, newc_o[...], ((0,), (0,)))
    total = exact_dot(burd_o[...], turn, ((1,), (0,)))
    sburd_ref[...] = total[:2]
    cburd_ref[...] = total[2:3]

    @pl.loop(0, news_o.shape[1], unroll=8)
    def _(k):
        at = order_ref[k]
        for g in range(2):
            news_ref[g, at] = news_o[g, k]


def step_kernel(
    ncol, npar, blocks, width, total_cells,
    rate_ref, conc_ref, emis_ref, sens_ref, src_ref, cx_ref, ux_ref, cy_ref, uy_ref,
    newc_ref, news_ref, burd_ref,
    conc_in, conc_rows, emis_rows, newc_rows, invc, lu, mid, coef,
    send1, send2, halo1, halo2, part, cpart, cpart_in, tot_out, tot_in,
    face_c, face_u, conc_ssem, conc_rsem, f_ssem, f_rsem, h_ssem, h_rsem, cp_ssem, cp_rsem, t_ssem, t_rsem,
):
    species = blocks * width
    pairs = width // 2
    half = SUB // 2
    col, par = (lax.axis_index("cols"), lax.axis_index("params"))
    rows = conc_ref.shape[1] // 128
    has_left, has_right = (col > 0, col < ncol - 1)

    barrier = pltpu.get_barrier_semaphore()
    for d in range(1, ncol):
        pl.semaphore_signal(barrier, inc=1, device_id=(lax.rem(col + d, ncol), par), device_id_type=MESH)
    for d in range(1, npar):
        pl.semaphore_signal(barrier, inc=1, device_id=(col, lax.rem(par + d, npar)), device_id_type=MESH)

    row = lax.broadcasted_iota(jnp.int32, (SUB, 128), 0)
    lane = lax.broadcasted_iota(jnp.int32, (SUB, 128), 1)
    top = row < half

    @pl.when(jnp.logical_not(has_left))
    def _():
        halo1[0] = jnp.zeros_like(halo1[0])
        halo2[0] = jnp.zeros_like(halo2[0])

    @pl.when(jnp.logical_not(has_right))
    def _():
        halo1[1] = jnp.zeros_like(halo1[1])
        halo2[1] = jnp.zeros_like(halo2[1])
        face_c[...] = jnp.zeros_like(face_c)
        face_u[...] = jnp.zeros_like(face_u)

    def face_copies():
        def one(src, dst, at):
            return pltpu.make_async_remote_copy(
                src_ref=src, dst_ref=dst, send_sem=f_ssem.at[at], recv_sem=f_rsem.at[at],
                device_id=(jnp.maximum(col - 1, 0), par), device_id_type=MESH,
            )

        return (one(cx_ref, face_c, 0), one(ux_ref, face_u, 1))

    def set_coefficients():
        @pl.when(has_right)
        def _():
            for copy in face_copies():
                copy.wait_recv()

        cx, cy = (cx_ref[...], cy_ref[...])
        ux, uy = (ux_ref[...] == 1, uy_ref[...] == 1)
        zero = jnp.zeros_like(cx)
        in_x, out_x = (jnp.where(ux, cx, zero), jnp.where(ux, zero, cx))
        in_y, out_y = (jnp.where(uy, cy, zero), jnp.where(uy, zero, cy))
        face = pltpu.roll(face_c[...], half, 0)
        up = pltpu.roll(face_u[...], half, 0) == 1
        in_x_face, out_x_face = (jnp.where(up, face, zero), jnp.where(up, zero, face))
        next_in_x = jnp.where(top, pltpu.roll(in_x, half, 0), in_x_face)
        next_out_x = jnp.where(top, pltpu.roll(out_x, half, 0), out_x_face)
        last = lane == 127
        next_in_y = jnp.where(last, zero, pltpu.roll(in_y, 127, 1))
        next_out_y = jnp.where(last, zero, pltpu.roll(out_y, 127, 1))
        coef[0] = 1.0 - (out_x + next_in_x) - (out_y + next_in_y)
        coef[1] = jnp.where(jnp.logical_and(top, jnp.logical_not(has_left)), zero, in_x)
        coef[2] = next_out_x
        coef[3] = jnp.where(lane == 0, zero, in_y)
        coef[4] = next_out_y

    def pack_pair(send, b, k, first, second):
        turned = [pltpu.roll(value, half, 0) for value in first]
        ahead = [jnp.where(top, turned[g], second[g]) for g in range(2)]
        behind = [jnp.where(top, second[g], turned[g]) for g in range(2)]
        send[0, b, k] = jnp.concatenate(ahead, axis=0).astype(jnp.bfloat16)
        send[1, b, k] = jnp.concatenate(behind, axis=0).astype(jnp.bfloat16)

    def halo_copy(which, way, b):
        send, halo = ((send1, halo1), (send2, halo2))[which]
        target = jnp.minimum(col + 1, ncol - 1) if way == 0 else jnp.maximum(col - 1, 0)
        return pltpu.make_async_remote_copy(
            src_ref=send.at[way, b], dst_ref=halo.at[way, b],
            send_sem=h_ssem.at[which, way, b], recv_sem=h_rsem.at[which, way, b],
            device_id=(target, par), device_id_type=MESH,
        )

    def start_halo(which, b):
        @pl.when(has_right)
        def _():
            halo_copy(which, 0, b).start()

        @pl.when(has_left)
        def _():
            halo_copy(which, 1, b).start()

    def wait_halo(which, b):
        @pl.when(has_left)
        def _():
            halo_copy(which, 0, b).wait_recv()

        @pl.when(has_right)
        def _():
            halo_copy(which, 1, b).wait_recv()

    def halo_pair(halo, b, k):
        from_left = halo[0, b, k].astype(jnp.float32)
        from_right = halo[1, b, k].astype(jnp.float32)
        first, second = ([], [])
        for g in range(2):
            low, high = (from_left[g * SUB:(g + 1) * SUB], from_right[g * SUB:(g + 1) * SUB])
            first.append(jnp.where(top, low, high))
            second.append(pltpu.roll(jnp.where(top, high, low), half, 0))
        return (first, second)

    def advance(s, h):
        a0, al, ar, ad, au = (coef[n] for n in range(5))
        turned = pltpu.roll(s, half, 0)
        before_x = jnp.where(top, h, turned)
        after_x = jnp.where(top, turned, h)
        return (
            a0 * s + al * before_x + ar * after_x
            + ad * pltpu.roll(s, 1, 1) + au * pltpu.roll(s, 127, 1)
        )

    def pack_first(b):
        for k in range(pairs):
            i, j = (b * width + 2 * k, b * width + 2 * k + 1)
            pack_pair(send1, b, k, (sens_ref[0, i], sens_ref[1, i]), (sens_ref[0, j], sens_ref[1, j]))

    pack_first(0)
    pl.semaphore_wait(barrier, ncol - 1 + npar - 1)

    @pl.when(has_left)
    def _():
        for copy in face_copies():
            copy.start()

    conc_copies = []
    for d in range(1, npar):
        copy = pltpu.make_async_remote_copy(
            src_ref=conc_ref, dst_ref=conc_in.at[npar - 1 - d],
            send_sem=conc_ssem.at[d - 1], recv_sem=conc_rsem.at[npar - 1 - d],
            device_id=(col, lax.rem(par + d, npar)), device_id_type=MESH,
        )
        copy.start()
        conc_copies.append(copy)

    @pl.loop(1, blocks)
    def _(b):
        pack_first(b)
        start_halo(0, b - 1)

    def spread(read, target, base):
        @pl.loop(0, species // SUB)
        def _(t):
            for r in range(rows):
                target[pl.ds(t * SUB * SUB + base + r, SUB, stride=SUB), :] = read(t, r)

    def own(ref):
        return lambda t, r: ref[pl.ds(pl.multiple_of(t * SUB, SUB), SUB), r * 128:(r + 1) * 128]

    spread(own(conc_ref), conc_rows, par * rows)
    start_halo(0, blocks - 1)
    spread(own(emis_ref), emis_rows, par * rows)
    for d in range(1, npar):
        conc_copies[npar - 1 - d].wait_recv()
        spread(own(conc_in.at[d - 1]), conc_rows, lax.rem(par + d, npar) * rows)

    set_coefficients()

    def tile(ref, index):
        return ref[pl.ds(pl.multiple_of(index * SUB, SUB), SUB), :]

    def factorize(b):
        c = [tile(conc_rows, b * width + j) for j in range(width)]
        for i in range(width):
            invc[b, i] = 1.0 / c[i]

        def fresh(i):
            rates = [rate_ref[b, i * width + j] for j in range(width)]
            total = rates[0] * c[0]
            for j in range(1, width):
                total = total + rates[j] * c[j]
            diagonal = (1.0 + total) * invc[b, i] - rates[i]
            return [diagonal if j == i else jnp.full((SUB, 128), -rates[j], jnp.float32) for j in range(width)]

        for i in range(0, width, 2):
            x, y = (fresh(i), fresh(i + 1))
            for k in range(i):
                inv = lu[b, k, k]
                lx, ly = (x[k] * inv, y[k] * inv)
                lu[b, i, k] = lx
                lu[b, i + 1, k] = ly
                for j in range(k + 1, width):
                    u = lu[b, k, j]
                    x[j] = x[j] - lx * u
                    y[j] = y[j] - ly * u
            inv = 1.0 / x[i]
            lu[b, i, i] = inv
            ly = y[i] * inv
            lu[b, i + 1, i] = ly
            for j in range(i + 1, width):
                lu[b, i, j] = x[j]
                y[j] = y[j] - ly * x[j]
            lu[b, i + 1, i + 1] = 1.0 / y[i + 1]
            for j in range(i + 2, width):
                lu[b, i + 1, j] = y[j]

    def solve(b, sides):
        sides = [list(side) for side in sides]
        for k in range(width):
            for i in range(k + 1, width):
                low = lu[b, i, k]
                for side in sides:
                    side[i] = side[i] - low * side[k]
        for k in range(width - 1, -1, -1):
            inv = lu[b, k, k]
            for side in sides:
                side[k] = side[k] * inv
            for i in range(k):
                up = lu[b, i, k]
                for side in sides:
                    side[i] = side[i] - up * side[k]
        return [[side[k] * invc[b, k] for k in range(width)] for side in sides]

    @pl.loop(0, blocks)
    def _(b):
        factorize(b)
        wait_halo(0, b)
        for k in range(pairs):
            i, j = (b * width + 2 * k, b * width + 2 * k + 1)
            h_first, h_second = halo_pair(halo1, b, k)
            first = [advance(sens_ref[g, i], h_first[g]) for g in range(2)]
            second = [advance(sens_ref[g, j], h_second[g]) for g in range(2)]
            for g in range(2):
                mid[g, b, 2 * k] = first[g]
                mid[g, b, 2 * k + 1] = second[g]
            pack_pair(send2, b, k, first, second)
        base = []
        for k in range(width):
            o = b * width + k
            base.append(tile(conc_rows, o) + tile(emis_rows, o))
        (base,) = solve(b, [base])
        for k in range(width):
            o = b * width + k
            newc_rows[pl.ds(pl.multiple_of(o * SUB, SUB), SUB), :] = base[k]
        start_halo(1, b)

    @pl.loop(0, species // SUB)
    def _(t):
        total = jnp.zeros((SUB, 128), jnp.float32)
        at = pl.ds(pl.multiple_of(t * SUB, SUB), SUB)
        for r in range(rows):
            value = newc_rows[pl.ds(t * SUB * SUB + par * rows + r, SUB, stride=SUB), :]
            newc_ref[at, r * 128:(r + 1) * 128] = value
            total = total + value
        part[0, at, :] = total

    ones = jnp.ones((SUB, 128), jnp.float32)

    def lane_sums(value):
        return lax.dot_general(
            ones, value, (((1,), (1,)), ((), ())),
            precision=lax.Precision.HIGHEST, preferred_element_type=jnp.float32,
        )

    own_c = lane_sums(part[0])
    cpart[...] = own_c
    cpart_in[par] = own_c

    def second_half(b):
        wait_halo(1, b)
        sides = [[], []]
        for k in range(pairs):
            i, j = (b * width + 2 * k, b * width + 2 * k + 1)
            h_first, h_second = halo_pair(halo2, b, k)
            for g in range(2):
                sides[g].append(advance(mid[g, b, 2 * k], h_first[g]) + src_ref[g, i].astype(jnp.float32))
                sides[g].append(advance(mid[g, b, 2 * k + 1], h_second[g]) + src_ref[g, j].astype(jnp.float32))
        sides = solve(b, sides)
        for g in range(2):
            for k in range(width):
                at = (g * species + b * width + k) * SUB
                news_ref[pl.ds(pl.multiple_of(at, SUB), SUB), :] = sides[g][k]

    def cpart_copy(d):
        return pltpu.make_async_remote_copy(
            src_ref=cpart, dst_ref=cpart_in.at[par],
            send_sem=cp_ssem.at[d - 1], recv_sem=cp_rsem.at[d - 1],
            device_id=(col, lax.rem(par + d, npar)), device_id_type=MESH,
        )

    @pl.loop(0, blocks)
    def _(b):
        second_half(b)

        @pl.when(b == 0)
        def _():
            for d in range(1, npar):
                cpart_copy(d).start()

    @pl.loop(0, species // SUB)
    def _(t):
        at = pl.ds(pl.multiple_of(t * SUB, SUB), SUB)
        for g in range(2):
            total = jnp.zeros((SUB, 128), jnp.float32)
            for r in range(SUB):
                total = total + news_ref[pl.ds(g * species * SUB + t * SUB * SUB + r, SUB, stride=SUB), :]
            part[1 + g, at, :] = total

    for d in range(1, npar):
        cpart_copy(d).wait()
    c_total = cpart_in[0]
    for q in range(1, npar):
        c_total = c_total + cpart_in[q]
    sums = [lane_sums(part[1 + g]) for g in range(2)]
    result = jnp.where(row == 0, sums[0], jnp.where(row == 1, sums[1], c_total))
    tot_out[...] = result
    tot_in[col] = result
    for d in range(1, npar):
        conc_copies[d - 1].wait_send()

    @pl.when(has_left)
    def _():
        for copy in face_copies():
            copy.wait_send()

    @pl.loop(0, blocks)
    def _(b):
        for which in range(2):
            @pl.when(has_right)
            def _():
                halo_copy(which, 0, b).wait_send()

            @pl.when(has_left)
            def _():
                halo_copy(which, 1, b).wait_send()

    totals = []
    for d in range(1, ncol):
        copy = pltpu.make_async_remote_copy(
            src_ref=tot_out, dst_ref=tot_in.at[col],
            send_sem=t_ssem.at[d - 1], recv_sem=t_rsem.at[d - 1],
            device_id=(lax.rem(col + d, ncol), par), device_id_type=MESH,
        )
        copy.start()
        totals.append(copy)
    for copy in totals:
        copy.wait()
    total = tot_in[0]
    for q in range(1, ncol):
        total = total + tot_in[q]
    total = total / total_cells
    burd_ref[...] = total


def shards(
    concentration, emissions, rate_table, species_order, sensitivity, source_terms,
    courant_x, upwind_x, courant_y, upwind_y,
):
    ncol, npar = (lax.axis_size("cols"), lax.axis_size("params"))
    blocks, width = (rate_table.shape[0], rate_table.shape[1])
    groups, species, planes, layers, across = sensitivity.shape
    tall = planes * layers
    assert groups == 2 and tall == SUB and planes == 2 and across == 128
    cells = tall * across
    pairs = width // 2

    vm = pltpu.VMEM
    dma = pltpu.SemaphoreType.DMA
    rows_shape = (species * SUB, 128)
    packed_shape = (2, blocks, pairs, 2 * SUB, 128)
    in_vmem = pl.BlockSpec(memory_space=pltpu.VMEM)
    in_smem = pl.BlockSpec(memory_space=pltpu.SMEM)
    order_column = species_order.reshape(species, 1)
    limits = pltpu.CompilerParams(vmem_limit_bytes=16 * 1024 * 1024)
    stacked = (groups, species, SUB, across)
    conc_o, emis_o, sens_o, src_o = pl.pallas_call(
        order_kernel,
        out_shape=(
            jax.ShapeDtypeStruct(concentration.shape, jnp.float32),
            jax.ShapeDtypeStruct(concentration.shape, jnp.float32),
            jax.ShapeDtypeStruct(stacked, jnp.float32),
            jax.ShapeDtypeStruct(stacked, jnp.bfloat16),
        ),
        in_specs=[in_smem] + [in_vmem] * 5,
        out_specs=[in_vmem] * 4,
        compiler_params=limits,
    )(
        species_order, order_column, concentration, emissions,
        sensitivity.reshape(stacked), source_terms.reshape(stacked),
    )
    newc_o, news_o, burd_o = pl.pallas_call(
        functools.partial(step_kernel, ncol, npar, blocks, width, cells * ncol),
        out_shape=(
            jax.ShapeDtypeStruct(concentration.shape, jnp.float32),
            jax.ShapeDtypeStruct((groups * species * SUB, 128), jnp.float32),
            jax.ShapeDtypeStruct((SUB, species), jnp.float32),
        ),
        in_specs=[in_smem] + [in_vmem] * 8,
        out_specs=[in_vmem] * 3,
        scratch_shapes=[
            vm((npar - 1,) + concentration.shape, jnp.float32),
            vm(rows_shape, jnp.float32),
            vm(rows_shape, jnp.float32),
            vm(rows_shape, jnp.float32),
            vm((blocks, width, SUB, 128), jnp.float32),
            vm((blocks, width, width, SUB, 128), jnp.float32),
            vm((groups, blocks, width, SUB, 128), jnp.float32),
            vm((5, SUB, 128), jnp.float32),
            vm(packed_shape, jnp.bfloat16),
            vm(packed_shape, jnp.bfloat16),
            vm(packed_shape, jnp.bfloat16),
            vm(packed_shape, jnp.bfloat16),
            vm((3, species, 128), jnp.float32),
            vm((SUB, species), jnp.float32),
            vm((npar, SUB, species), jnp.float32),
            vm((SUB, species), jnp.float32),
            vm((ncol, SUB, species), jnp.float32),
            vm((SUB, 128), jnp.float32),
            vm((SUB, 128), jnp.int32),
            dma((npar - 1,)), dma((npar - 1,)),
            dma((2,)), dma((2,)),
            dma((2, 2, blocks)), dma((2, 2, blocks)),
            dma((npar - 1,)), dma((npar - 1,)),
            dma((ncol - 1,)), dma((ncol - 1,)),
        ],
        compiler_params=pltpu.CompilerParams(
            collective_id=0, has_side_effects=True, vmem_limit_bytes=48 * 1024 * 1024
        ),
    )(
        rate_table.reshape(blocks, width * width), conc_o, emis_o, sens_o, src_o,
        courant_x.reshape(SUB, across), upwind_x.reshape(SUB, across),
        courant_y.reshape(SUB, across), upwind_y.reshape(SUB, across),
    )
    newc, news, sburd, cburd = pl.pallas_call(
        restore_kernel,
        out_shape=(
            jax.ShapeDtypeStruct(concentration.shape, jnp.float32),
            jax.ShapeDtypeStruct(stacked, jnp.float32),
            jax.ShapeDtypeStruct((groups, species), jnp.float32),
            jax.ShapeDtypeStruct((1, species), jnp.float32),
        ),
        in_specs=[in_smem] + [in_vmem] * 4,
        out_specs=[in_vmem] * 4,
        compiler_params=limits,
    )(species_order, order_column, newc_o, news_o.reshape(stacked), burd_o)
    return (newc, news.reshape(sensitivity.shape), sburd, cburd.reshape(species))


def solution(mesh):
    in_specs = (
        P(None, ("cols", "params")),
        P(None, ("cols", "params")),
        P(),
        P(),
        P("params", None, "cols", None, None),
        P("params", None, "cols", None, None),
        P("cols", None, None),
        P("cols", None, None),
        P("cols", None, None),
        P("cols", None, None),
    )
    out_specs = (
        P(None, ("cols", "params")),
        P("params", None, "cols", None, None),
        P("params", None),
        P(),
    )
    return jax.shard_map(shards, mesh=mesh, in_specs=in_specs, out_specs=out_specs, check_vma=False)
```

```python
import functools
import jax
import jax.numpy as jnp
from jax import lax
from jax.experimental import pallas as pl
from jax.experimental.pallas import tpu as pltpu
from jax.sharding import PartitionSpec as P

MESH = pl.DeviceIdType.MESH
SUB = 8


def pinned(value):
    return pltpu.with_memory_space_constraint(value, pltpu.HBM)


def one_hot(column_ref):
    species = column_ref.shape[0]
    at = lax.broadcasted_iota(jnp.int32, (species, species), 1)
    return jnp.where(at == column_ref[...], 1.0, 0.0).astype(jnp.float32)


def exact_dot(left, right, over):
    return lax.dot_general(
        left, right, (over, ((), ())),
        precision=lax.Precision.HIGHEST, preferred_element_type=jnp.float32,
    )


def order_kernel(order_ref, column_ref, conc_hbm, emis_hbm, sens_hbm, src_hbm, conc_o, emis_o, sens_o, src_o, conc_ref, emis_ref, sens_ref, src_ref, sems):
    held = ((conc_hbm, conc_ref), (emis_hbm, emis_ref), (sens_hbm, sens_ref), (src_hbm, src_ref))
    copies = [pltpu.make_async_copy(src, dst, sems.at[n]) for n, (src, dst) in enumerate(held)]
    for copy in copies:
        copy.start()
    turn = one_hot(column_ref)
    copies[0].wait()
    conc_o[...] = exact_dot(turn, conc_ref[...], ((1,), (0,)))
    copies[1].wait()
    emis_o[...] = exact_dot(turn, emis_ref[...], ((1,), (0,)))
    copies[2].wait()
    copies[3].wait()

    @pl.loop(0, sens_ref.shape[1], unroll=8)
    def _(k):
        at = order_ref[k]
        for g in range(2):
            sens_o[g, k] = sens_ref[g, at]
            src_o[g, k] = src_ref[g, at]


def restore_kernel(order_ref, column_ref, newc_o, news_o, burd_o, newc_ref, news_ref, sburd_ref, cburd_ref):
    turn = one_hot(column_ref)
    newc_ref[...] = exact_dot(turn, newc_o[...], ((0,), (0,)))
    total = exact_dot(burd_o[...], turn, ((1,), (0,)))
    sburd_ref[...] = total[:2]
    cburd_ref[...] = total[2:3]

    @pl.loop(0, news_o.shape[1], unroll=8)
    def _(k):
        at = order_ref[k]
        for g in range(2):
            news_ref[g, at] = news_o[g, k]


def step_kernel(
    ncol, npar, blocks, width, total_cells,
    rate_ref, conc_ref, emis_ref, sens_ref, src_ref, cx_ref, ux_ref, cy_ref, uy_ref,
    newc_ref, news_ref, burd_ref,
    conc_in, conc_rows, emis_rows, newc_rows, invc, lu, mid, coef,
    send1, send2, halo1, halo2, part, cpart, cpart_in, tot_out, tot_in,
    face_c, face_u, conc_ssem, conc_rsem, f_ssem, f_rsem, h_ssem, h_rsem, cp_ssem, cp_rsem, t_ssem, t_rsem,
):
    species = blocks * width
    pairs = width // 2
    half = SUB // 2
    col, par = (lax.axis_index("cols"), lax.axis_index("params"))
    rows = conc_ref.shape[1] // 128
    has_left, has_right = (col > 0, col < ncol - 1)

    barrier = pltpu.get_barrier_semaphore()
    for d in range(1, ncol):
        pl.semaphore_signal(barrier, inc=1, device_id=(lax.rem(col + d, ncol), par), device_id_type=MESH)
    for d in range(1, npar):
        pl.semaphore_signal(barrier, inc=1, device_id=(col, lax.rem(par + d, npar)), device_id_type=MESH)

    row = lax.broadcasted_iota(jnp.int32, (SUB, 128), 0)
    lane = lax.broadcasted_iota(jnp.int32, (SUB, 128), 1)
    top = row < half

    @pl.when(jnp.logical_not(has_left))
    def _():
        halo1[0] = jnp.zeros_like(halo1[0])
        halo2[0] = jnp.zeros_like(halo2[0])

    @pl.when(jnp.logical_not(has_right))
    def _():
        halo1[1] = jnp.zeros_like(halo1[1])
        halo2[1] = jnp.zeros_like(halo2[1])
        face_c[...] = jnp.zeros_like(face_c)
        face_u[...] = jnp.zeros_like(face_u)

    def face_copies():
        def one(src, dst, at):
            return pltpu.make_async_remote_copy(
                src_ref=src, dst_ref=dst, send_sem=f_ssem.at[at], recv_sem=f_rsem.at[at],
                device_id=(jnp.maximum(col - 1, 0), par), device_id_type=MESH,
            )

        return (one(cx_ref, face_c, 0), one(ux_ref, face_u, 1))

    def set_coefficients():
        @pl.when(has_right)
        def _():
            for copy in face_copies():
                copy.wait_recv()

        cx, cy = (cx_ref[...], cy_ref[...])
        ux, uy = (ux_ref[...] == 1, uy_ref[...] == 1)
        zero = jnp.zeros_like(cx)
        in_x, out_x = (jnp.where(ux, cx, zero), jnp.where(ux, zero, cx))
        in_y, out_y = (jnp.where(uy, cy, zero), jnp.where(uy, zero, cy))
        face = pltpu.roll(face_c[...], half, 0)
        up = pltpu.roll(face_u[...], half, 0) == 1
        in_x_face, out_x_face = (jnp.where(up, face, zero), jnp.where(up, zero, face))
        next_in_x = jnp.where(top, pltpu.roll(in_x, half, 0), in_x_face)
        next_out_x = jnp.where(top, pltpu.roll(out_x, half, 0), out_x_face)
        last = lane == 127
        next_in_y = jnp.where(last, zero, pltpu.roll(in_y, 127, 1))
        next_out_y = jnp.where(last, zero, pltpu.roll(out_y, 127, 1))
        coef[0] = 1.0 - (out_x + next_in_x) - (out_y + next_in_y)
        coef[1] = jnp.where(jnp.logical_and(top, jnp.logical_not(has_left)), zero, in_x)
        coef[2] = next_out_x
        coef[3] = jnp.where(lane == 0, zero, in_y)
        coef[4] = next_out_y

    def pack_pair(send, b, k, first, second):
        turned = [pltpu.roll(value, half, 0) for value in first]
        ahead = [jnp.where(top, turned[g], second[g]) for g in range(2)]
        behind = [jnp.where(top, second[g], turned[g]) for g in range(2)]
        send[0, b, k] = jnp.concatenate(ahead, axis=0).astype(jnp.bfloat16)
        send[1, b, k] = jnp.concatenate(behind, axis=0).astype(jnp.bfloat16)

    def halo_copy(which, way, b):
        send, halo = ((send1, halo1), (send2, halo2))[which]
        target = jnp.minimum(col + 1, ncol - 1) if way == 0 else jnp.maximum(col - 1, 0)
        return pltpu.make_async_remote_copy(
            src_ref=send.at[way, b], dst_ref=halo.at[way, b],
            send_sem=h_ssem.at[which, way, b], recv_sem=h_rsem.at[which, way, b],
            device_id=(target, par), device_id_type=MESH,
        )

    def start_halo(which, b):
        @pl.when(has_right)
        def _():
            halo_copy(which, 0, b).start()

        @pl.when(has_left)
        def _():
            halo_copy(which, 1, b).start()

    def wait_halo(which, b):
        @pl.when(has_left)
        def _():
            halo_copy(which, 0, b).wait_recv()

        @pl.when(has_right)
        def _():
            halo_copy(which, 1, b).wait_recv()

    def halo_pair(halo, b, k):
        from_left = halo[0, b, k].astype(jnp.float32)
        from_right = halo[1, b, k].astype(jnp.float32)
        first, second = ([], [])
        for g in range(2):
            low, high = (from_left[g * SUB:(g + 1) * SUB], from_right[g * SUB:(g + 1) * SUB])
            first.append(jnp.where(top, low, high))
            second.append(pltpu.roll(jnp.where(top, high, low), half, 0))
        return (first, second)

    def advance(s, h):
        a0, al, ar, ad, au = (coef[n] for n in range(5))
        turned = pltpu.roll(s, half, 0)
        before_x = jnp.where(top, h, turned)
        after_x = jnp.where(top, turned, h)
        return (
            a0 * s + al * before_x + ar * after_x
            + ad * pltpu.roll(s, 1, 1) + au * pltpu.roll(s, 127, 1)
        )

    def pack_first(b):
        for k in range(pairs):
            i, j = (b * width + 2 * k, b * width + 2 * k + 1)
            pack_pair(send1, b, k, (sens_ref[0, i], sens_ref[1, i]), (sens_ref[0, j], sens_ref[1, j]))

    pack_first(0)
    pl.semaphore_wait(barrier, ncol - 1 + npar - 1)

    @pl.when(has_left)
    def _():
        for copy in face_copies():
            copy.start()

    conc_copies = []
    for d in range(1, npar):
        copy = pltpu.make_async_remote_copy(
            src_ref=conc_ref, dst_ref=conc_in.at[npar - 1 - d],
            send_sem=conc_ssem.at[d - 1], recv_sem=conc_rsem.at[npar - 1 - d],
            device_id=(col, lax.rem(par + d, npar)), device_id_type=MESH,
        )
        copy.start()
        conc_copies.append(copy)

    @pl.loop(1, blocks)
    def _(b):
        pack_first(b)
        start_halo(0, b - 1)

    def spread(read, target, base):
        @pl.loop(0, species // SUB)
        def _(t):
            for r in range(rows):
                target[pl.ds(t * SUB * SUB + base + r, SUB, stride=SUB), :] = read(t, r)

    def own(ref):
        return lambda t, r: ref[pl.ds(pl.multiple_of(t * SUB, SUB), SUB), r * 128:(r + 1) * 128]

    spread(own(conc_ref), conc_rows, par * rows)
    start_halo(0, blocks - 1)
    spread(own(emis_ref), emis_rows, par * rows)
    for d in range(1, npar):
        conc_copies[npar - 1 - d].wait_recv()
        spread(own(conc_in.at[d - 1]), conc_rows, lax.rem(par + d, npar) * rows)

    set_coefficients()

    def tile(ref, index):
        return ref[pl.ds(pl.multiple_of(index * SUB, SUB), SUB), :]

    def factorize(b):
        c = [tile(conc_rows, b * width + j) for j in range(width)]
        for i in range(width):
            invc[b, i] = 1.0 / c[i]

        def fresh(i):
            rates = [rate_ref[b, i * width + j] for j in range(width)]
            total = rates[0] * c[0]
            for j in range(1, width):
                total = total + rates[j] * c[j]
            diagonal = (1.0 + total) * invc[b, i] - rates[i]
            return [diagonal if j == i else jnp.full((SUB, 128), -rates[j], jnp.float32) for j in range(width)]

        for i in range(0, width, 2):
            x, y = (fresh(i), fresh(i + 1))
            for k in range(i):
                inv = lu[b, k, k]
                lx, ly = (x[k] * inv, y[k] * inv)
                lu[b, i, k] = lx
                lu[b, i + 1, k] = ly
                for j in range(k + 1, width):
                    u = lu[b, k, j]
                    x[j] = x[j] - lx * u
                    y[j] = y[j] - ly * u
            inv = 1.0 / x[i]
            lu[b, i, i] = inv
            ly = y[i] * inv
            lu[b, i + 1, i] = ly
            for j in range(i + 1, width):
                lu[b, i, j] = x[j]
                y[j] = y[j] - ly * x[j]
            lu[b, i + 1, i + 1] = 1.0 / y[i + 1]
            for j in range(i + 2, width):
                lu[b, i + 1, j] = y[j]

    def solve(b, sides):
        sides = [list(side) for side in sides]
        for k in range(width):
            for i in range(k + 1, width):
                low = lu[b, i, k]
                for side in sides:
                    side[i] = side[i] - low * side[k]
        for k in range(width - 1, -1, -1):
            inv = lu[b, k, k]
            for side in sides:
                side[k] = side[k] * inv
            for i in range(k):
                up = lu[b, i, k]
                for side in sides:
                    side[i] = side[i] - up * side[k]
        return [[side[k] * invc[b, k] for k in range(width)] for side in sides]

    @pl.loop(0, blocks)
    def _(b):
        factorize(b)
        wait_halo(0, b)
        for k in range(pairs):
            i, j = (b * width + 2 * k, b * width + 2 * k + 1)
            h_first, h_second = halo_pair(halo1, b, k)
            first = [advance(sens_ref[g, i], h_first[g]) for g in range(2)]
            second = [advance(sens_ref[g, j], h_second[g]) for g in range(2)]
            for g in range(2):
                mid[g, b, 2 * k] = first[g]
                mid[g, b, 2 * k + 1] = second[g]
            pack_pair(send2, b, k, first, second)
        base = []
        for k in range(width):
            o = b * width + k
            base.append(tile(conc_rows, o) + tile(emis_rows, o))
        (base,) = solve(b, [base])
        for k in range(width):
            o = b * width + k
            newc_rows[pl.ds(pl.multiple_of(o * SUB, SUB), SUB), :] = base[k]
        start_halo(1, b)

    @pl.loop(0, species // SUB)
    def _(t):
        total = jnp.zeros((SUB, 128), jnp.float32)
        at = pl.ds(pl.multiple_of(t * SUB, SUB), SUB)
        for r in range(rows):
            value = newc_rows[pl.ds(t * SUB * SUB + par * rows + r, SUB, stride=SUB), :]
            newc_ref[at, r * 128:(r + 1) * 128] = value
            total = total + value
        part[0, at, :] = total

    ones = jnp.ones((SUB, 128), jnp.float32)

    def lane_sums(value):
        return lax.dot_general(
            ones, value, (((1,), (1,)), ((), ())),
            precision=lax.Precision.HIGHEST, preferred_element_type=jnp.float32,
        )

    own_c = lane_sums(part[0])
    cpart[...] = own_c
    cpart_in[par] = own_c

    def second_half(b):
        wait_halo(1, b)
        sides = [[], []]
        for k in range(pairs):
            i, j = (b * width + 2 * k, b * width + 2 * k + 1)
            h_first, h_second = halo_pair(halo2, b, k)
            for g in range(2):
                sides[g].append(advance(mid[g, b, 2 * k], h_first[g]) + src_ref[g, i].astype(jnp.float32))
                sides[g].append(advance(mid[g, b, 2 * k + 1], h_second[g]) + src_ref[g, j].astype(jnp.float32))
        sides = solve(b, sides)
        for g in range(2):
            for k in range(width):
                at = (g * species + b * width + k) * SUB
                news_ref[pl.ds(pl.multiple_of(at, SUB), SUB), :] = sides[g][k]

    def cpart_copy(d):
        return pltpu.make_async_remote_copy(
            src_ref=cpart, dst_ref=cpart_in.at[par],
            send_sem=cp_ssem.at[d - 1], recv_sem=cp_rsem.at[d - 1],
            device_id=(col, lax.rem(par + d, npar)), device_id_type=MESH,
        )

    @pl.loop(0, blocks)
    def _(b):
        second_half(b)

        @pl.when(b == 0)
        def _():
            for d in range(1, npar):
                cpart_copy(d).start()

    @pl.loop(0, species // SUB)
    def _(t):
        at = pl.ds(pl.multiple_of(t * SUB, SUB), SUB)
        for g in range(2):
            total = jnp.zeros((SUB, 128), jnp.float32)
            for r in range(SUB):
                total = total + news_ref[pl.ds(g * species * SUB + t * SUB * SUB + r, SUB, stride=SUB), :]
            part[1 + g, at, :] = total

    for d in range(1, npar):
        cpart_copy(d).wait()
    c_total = cpart_in[0]
    for q in range(1, npar):
        c_total = c_total + cpart_in[q]
    sums = [lane_sums(part[1 + g]) for g in range(2)]
    result = jnp.where(row == 0, sums[0], jnp.where(row == 1, sums[1], c_total))
    tot_out[...] = result
    tot_in[col] = result
    for d in range(1, npar):
        conc_copies[d - 1].wait_send()

    @pl.when(has_left)
    def _():
        for copy in face_copies():
            copy.wait_send()

    @pl.loop(0, blocks)
    def _(b):
        for which in range(2):
            @pl.when(has_right)
            def _():
                halo_copy(which, 0, b).wait_send()

            @pl.when(has_left)
            def _():
                halo_copy(which, 1, b).wait_send()

    totals = []
    for d in range(1, ncol):
        copy = pltpu.make_async_remote_copy(
            src_ref=tot_out, dst_ref=tot_in.at[col],
            send_sem=t_ssem.at[d - 1], recv_sem=t_rsem.at[d - 1],
            device_id=(lax.rem(col + d, ncol), par), device_id_type=MESH,
        )
        copy.start()
        totals.append(copy)
    for copy in totals:
        copy.wait()
    total = tot_in[0]
    for q in range(1, ncol):
        total = total + tot_in[q]
    total = total / total_cells
    burd_ref[...] = total


def shards(
    concentration, emissions, rate_table, species_order, sensitivity, source_terms,
    courant_x, upwind_x, courant_y, upwind_y,
):
    ncol, npar = (lax.axis_size("cols"), lax.axis_size("params"))
    blocks, width = (rate_table.shape[0], rate_table.shape[1])
    groups, species, planes, layers, across = sensitivity.shape
    tall = planes * layers
    assert groups == 2 and tall == SUB and planes == 2 and across == 128
    cells = tall * across
    pairs = width // 2

    vm = pltpu.VMEM
    dma = pltpu.SemaphoreType.DMA
    rows_shape = (species * SUB, 128)
    packed_shape = (2, blocks, pairs, 2 * SUB, 128)
    in_vmem = pl.BlockSpec(memory_space=pltpu.VMEM)
    in_smem = pl.BlockSpec(memory_space=pltpu.SMEM)
    order_column = species_order.reshape(species, 1)
    limits = pltpu.CompilerParams(vmem_limit_bytes=16 * 1024 * 1024)
    stacked = (groups, species, SUB, across)
    conc_o, emis_o, sens_o, src_o = pl.pallas_call(
        order_kernel,
        out_shape=(
            jax.ShapeDtypeStruct(concentration.shape, jnp.float32),
            jax.ShapeDtypeStruct(concentration.shape, jnp.float32),
            jax.ShapeDtypeStruct(stacked, jnp.float32),
            jax.ShapeDtypeStruct(stacked, jnp.bfloat16),
        ),
        in_specs=[in_smem, in_vmem] + [pl.BlockSpec(memory_space=pltpu.HBM)] * 4,
        out_specs=[in_vmem] * 4,
        scratch_shapes=[
            vm(concentration.shape, jnp.float32),
            vm(concentration.shape, jnp.float32),
            vm(stacked, jnp.float32),
            vm(stacked, jnp.bfloat16),
            dma((4,)),
        ],
        compiler_params=limits,
    )(
        species_order, order_column, pinned(concentration), pinned(emissions),
        pinned(sensitivity.reshape(stacked)), pinned(source_terms.reshape(stacked)),
    )
    newc_o, news_o, burd_o = pl.pallas_call(
        functools.partial(step_kernel, ncol, npar, blocks, width, cells * ncol),
        out_shape=(
            jax.ShapeDtypeStruct(concentration.shape, jnp.float32),
            jax.ShapeDtypeStruct((groups * species * SUB, 128), jnp.float32),
            jax.ShapeDtypeStruct((SUB, species), jnp.float32),
        ),
        in_specs=[in_smem] + [in_vmem] * 8,
        out_specs=[in_vmem] * 3,
        scratch_shapes=[
            vm((npar - 1,) + concentration.shape, jnp.float32),
            vm(rows_shape, jnp.float32),
            vm(rows_shape, jnp.float32),
            vm(rows_shape, jnp.float32),
            vm((blocks, width, SUB, 128), jnp.float32),
            vm((blocks, width, width, SUB, 128), jnp.float32),
            vm((groups, blocks, width, SUB, 128), jnp.float32),
            vm((5, SUB, 128), jnp.float32),
            vm(packed_shape, jnp.bfloat16),
            vm(packed_shape, jnp.bfloat16),
            vm(packed_shape, jnp.bfloat16),
            vm(packed_shape, jnp.bfloat16),
            vm((3, species, 128), jnp.float32),
            vm((SUB, species), jnp.float32),
            vm((npar, SUB, species), jnp.float32),
            vm((SUB, species), jnp.float32),
            vm((ncol, SUB, species), jnp.float32),
            vm((SUB, 128), jnp.float32),
            vm((SUB, 128), jnp.int32),
            dma((npar - 1,)), dma((npar - 1,)),
            dma((2,)), dma((2,)),
            dma((2, 2, blocks)), dma((2, 2, blocks)),
            dma((npar - 1,)), dma((npar - 1,)),
            dma((ncol - 1,)), dma((ncol - 1,)),
        ],
        compiler_params=pltpu.CompilerParams(
            collective_id=0, has_side_effects=True, vmem_limit_bytes=48 * 1024 * 1024
        ),
    )(
        rate_table.reshape(blocks, width * width), conc_o, emis_o, sens_o, src_o,
        courant_x.reshape(SUB, across), upwind_x.reshape(SUB, across),
        courant_y.reshape(SUB, across), upwind_y.reshape(SUB, across),
    )
    newc, news, sburd, cburd = pl.pallas_call(
        restore_kernel,
        out_shape=(
            jax.ShapeDtypeStruct(concentration.shape, jnp.float32),
            jax.ShapeDtypeStruct(stacked, jnp.float32),
            jax.ShapeDtypeStruct((groups, species), jnp.float32),
            jax.ShapeDtypeStruct((1, species), jnp.float32),
        ),
        in_specs=[in_smem] + [in_vmem] * 4,
        out_specs=[in_vmem] * 4,
        compiler_params=limits,
    )(species_order, order_column, newc_o, news_o.reshape(stacked), burd_o)
    return (newc, news.reshape(sensitivity.shape), sburd, cburd.reshape(species))


def solution(mesh):
    in_specs = (
        P(None, ("cols", "params")),
        P(None, ("cols", "params")),
        P(),
        P(),
        P("params", None, "cols", None, None),
        P("params", None, "cols", None, None),
        P("cols", None, None),
        P("cols", None, None),
        P("cols", None, None),
        P("cols", None, None),
    )
    out_specs = (
        P(None, ("cols", "params")),
        P("params", None, "cols", None, None),
        P("params", None),
        P(),
    )
    return jax.shard_map(shards, mesh=mesh, in_specs=in_specs, out_specs=out_specs, check_vma=False)
```
